32 devices in a mesh: gx: 8 (over z, x), pa: 4 (over y, core).
Axes of the slice: x: 2, y: 2, z: 4, core: 2. Of those that a mesh axis runs over, the one named last changes fastest.
Arguments:
- packed: float32 [2, 4096, 2048], P(None, 'gx', 'pa'), parts along dimension 2, may hold values from -6 to 6
- wave_y: int32 [2048], P('pa'), parts along dimension 0, may hold values from -2048 to 2047
- wave_z: int32 [2048], P('pa'), parts along dimension 0, may hold values from 1 to 2048
Outputs:
- spectra: float32 [2, 2, 4096, 2048], P(None, None, 'gx', 'pa'), parts along dimension 3
The draws below stay inside these ranges and needn't reach their ends.
There are 4 independent parts, one for each index of `pa`. The reference program is written for one: setup_inputs(seed, part) draws one part's arguments, and reference() takes and returns one part's arrays. A program takes and returns all parts, laid end to end along the dimension named above; each array names one. Nothing has to cross between parts.
All inputs are finite; a program needn't handle non-finite values.
Results may differ from the reference program's by a relative error of at most 0.00007.
Values sent between devices are 32-bit elements; how exact they have to be, the bound alone decides.
No kernel may reach another device: no remote copies, remote signals or barrier semaphores. Data moves between devices by JAX's collectives and lax.ppermute only.
A program may use at most 64 MiB of HBM per device.

```python
import math
import jax
import jax.numpy as jnp

NX = 4096
P_SIZE = 512


def touch_ends(values, own_key, least, top_value):
    place = [jax.random.randint(jax.random.fold_in(own_key, axis), (), 0, length) for axis, length in enumerate(values.shape)]
    widest = values.shape.index(max(values.shape))
    neighbour = place[:widest] + [(place[widest] + 1) % values.shape[widest]] + place[widest + 1:]
    return values.at[tuple(place)].set(least).at[tuple(neighbour)].set(top_value)


def shard_levels(rng, dims, split, least, top_value):
    level, own = 1.0, jax.random.fold_in(rng, 6)
    for axis_at, shards_of in split:
        heights = jnp.exp(jax.random.uniform(jax.random.fold_in(own, axis_at), (shards_of,), jnp.float32, least / len(split), top_value / len(split)))
        level = level * jnp.repeat(heights, dims[axis_at] // shards_of).reshape([-1 if axis == axis_at else 1 for axis in range(len(dims))])
    return level


def normal_values(rng, dims, scale, reach, split=(), kind=jnp.bfloat16):
    entries = scale * jax.random.normal(rng, dims, jnp.float32)
    if split:
        entries = entries * shard_levels(rng, dims, split, -0.22, 0.18)
    return jnp.clip(entries, -reach, reach).astype(kind)


def setup_inputs(seed: int = 0, part: int = 0) -> dict:
    key_of = jax.random.split(jax.random.key(seed), 4)
    part_splits = jax.random.split(jax.random.fold_in(key_of[3], part), 4)
    packed = normal_values(part_splits[0], (2, NX, P_SIZE), 1.0, 6.0, ((1, 8),), jnp.float32)
    wave_y = touch_ends(jax.random.randint(part_splits[1], (P_SIZE,), -(NX // 2), NX // 2), jax.random.fold_in(part_splits[1], 1), -(NX // 2), (NX // 2) - 1).astype(jnp.int32)
    wave_z = touch_ends(jax.random.randint(part_splits[2], (P_SIZE,), 1, NX // 2 + 1), jax.random.fold_in(part_splits[2], 1), 1, (NX // 2 + 1) - 1).astype(jnp.int32)
    return {"packed": packed, "wave_y": wave_y, "wave_z": wave_z}


def project(first_real, first_imag, back_real, back_imag, wave_ids, wave_y, wave_z):
    line_len = NX
    u_real = (first_real + back_real) / 2
    u_imag = (first_imag - back_imag) / 2
    v_real = (first_imag + back_imag) / 2
    v_imag = (back_real - first_real) / 2
    along_x = jnp.where(wave_ids < line_len // 2, wave_ids, wave_ids - line_len).astype(jnp.float32)[:, None]
    along_y = wave_y.astype(jnp.float32)[None, :]
    along_z = wave_z.astype(jnp.float32)[None, :]
    magnitude = along_x * along_x + along_y * along_y + along_z * along_z
    dot_real = (along_x * u_real + along_y * v_real) / magnitude
    dot_imag = (along_x * u_imag + along_y * v_imag) / magnitude
    first_comp = jnp.stack([u_real - along_x * dot_real, u_imag - along_x * dot_imag])
    second_comp = jnp.stack([v_real - along_y * dot_real, v_imag - along_y * dot_imag])
    return jnp.stack([first_comp, second_comp])

def reference(packed, wave_y, wave_z):
    field = packed[0] + 1j * packed[1]
    waves = jnp.fft.fft(field, axis=0) / math.sqrt(NX)
    mirror_field = jnp.roll(jnp.flip(waves, 0), 1, 0)
    wave_ids = jnp.arange(NX, dtype=jnp.int32)
    result = project(jnp.real(waves), jnp.imag(waves), jnp.real(mirror_field), jnp.imag(mirror_field), wave_ids, wave_y, wave_z)
    return result.astype(jnp.float32)
```

```python
import functools
import math

import jax
import jax.numpy as jnp
import ml_dtypes
import numpy as np
from jax import lax
from jax.experimental import pallas as pl
from jax.experimental.pallas import tpu as pltpu
from jax.sharding import PartitionSpec as P

NX = 4096
RADIX = 16
SUB = NX // RADIX
HALF_RADIX = RADIX // 2
HALF_LANES = 64
LANES = 2 * HALF_LANES
MIB = 1 << 20


def dft_tables():
    rows = np.arange(SUB)
    angles = 2.0 * np.pi * (rows[:, None] * rows[None, :] % SUB) / SUB
    matrix = np.concatenate([np.cos(angles), -np.sin(angles)]) / math.sqrt(NX)
    high = matrix.astype(np.float32).astype(ml_dtypes.bfloat16)
    low = (matrix - high.astype(np.float64)).astype(np.float32).astype(ml_dtypes.bfloat16)
    turn = 2.0 * np.pi * rows[:, None] * np.arange(RADIX)[None, :] / NX
    twiddle = np.concatenate([np.cos(turn), -np.sin(turn)], axis=1).astype(np.float32)
    return high, low, twiddle


def low_lanes(shape):
    return lax.broadcasted_iota(jnp.int32, shape, len(shape) - 1) < HALF_LANES


def swap_halves(value):
    return pltpu.roll(value, HALF_LANES, value.ndim - 1)


def pack_kernel(in_ref, out_ref):
    first, second = in_ref[0], in_ref[1]
    low = low_lanes(first.shape)
    even = jnp.where(low, first, swap_halves(second))
    odd = jnp.where(low, swap_halves(first), second)
    for side in range(2):
        out_ref[side, 0, 0] = even
        out_ref[side, 0, 1] = odd


def pack_lines(packed, chunk, side_size):
    block_len = packed.shape[1]
    tiles = side_size // 2
    rows = min(256, block_len)
    out = pl.pallas_call(
        pack_kernel,
        grid=(tiles, block_len // rows),
        in_specs=[pl.BlockSpec((2, rows, LANES), lambda t, r: (0, r, chunk * tiles + t))],
        out_specs=pl.BlockSpec((2, 1, 2, rows, LANES), lambda t, r: (0, t, 0, r, 0)),
        out_shape=jax.ShapeDtypeStruct((2, tiles, 2, block_len, LANES), jnp.float32),
        cost_estimate=pl.CostEstimate(
            flops=0, transcendentals=0, bytes_accessed=6 * side_size * block_len * LANES * 2
        ),
        name="pack_lines",
    )(packed)
    return out.reshape(2 * side_size, block_len, LANES)


def add(left, right):
    return left[0] + right[0], left[1] + right[1]


def sub(left, right):
    return left[0] - right[0], left[1] - right[1]


def turn_back(value):
    return value[1], -value[0]


def dft4(values):
    even_sum, even_dif = add(values[0], values[2]), sub(values[0], values[2])
    odd_sum, odd_dif = add(values[1], values[3]), turn_back(sub(values[1], values[3]))
    return [add(even_sum, odd_sum), add(even_dif, odd_dif), sub(even_sum, odd_sum), sub(even_dif, odd_dif)]


def dft8(values):
    root = math.sqrt(0.5)
    even, odd = dft4(values[0::2]), dft4(values[1::2])
    one = odd[1]
    three = odd[3]
    odd[1] = ((one[0] + one[1]) * root, (one[1] - one[0]) * root)
    odd[2] = turn_back(odd[2])
    odd[3] = ((three[1] - three[0]) * root, (three[0] + three[1]) * -root)
    return [add(e, o) for e, o in zip(even, odd)] + [sub(e, o) for e, o in zip(even, odd)]


def transform_kernel(meta_ref, wave_ref, high_ref, low_ref, twiddle_ref, line_ref, *rest, side_size):
    outs = rest[:side_size]
    split_high, split_low, product, result, sems = rest[side_size:]
    per_owner = HALF_RADIX // side_size
    for pair in range(RADIX // 2):
        columns = slice(2 * pair * LANES, 2 * (pair + 1) * LANES)
        for step in range(2):
            value = line_ref[pl.ds(2 * pair + step, SUB, stride=RADIX), :]
            high = value.astype(jnp.bfloat16)
            own = slice((2 * pair + step) * LANES, (2 * pair + step + 1) * LANES)
            split_high[:, own] = high
            split_low[:, own] = (value - high.astype(jnp.float32)).astype(jnp.bfloat16)
        dot = functools.partial(jnp.dot, preferred_element_type=jnp.float32)
        product[:, columns] = (
            dot(high_ref[...], split_high[:, columns])
            + dot(high_ref[...], split_low[:, columns])
            + dot(low_ref[...], split_high[:, columns])
        )

    own_place, side = meta_ref[0], meta_ref[1]
    side_float = side.astype(jnp.float32)
    sign = 1.0 - 2.0 * side_float
    along_y = jnp.broadcast_to(wave_ref[0:1, :], (8, LANES))
    cross = jnp.broadcast_to(wave_ref[1:2, :], (8, LANES))
    low = low_lanes((8, LANES))
    row_ids = lax.broadcasted_iota(jnp.int32, (8, LANES), 0).astype(jnp.float32) - 2048.0 * side_float

    def rows_body(step, carry):
        start = pl.multiple_of(step * 8, 8)
        twiddle = twiddle_ref[pl.ds(start, 8), :]
        turned = []
        for digit in range(RADIX):
            own = slice(digit * LANES, (digit + 1) * LANES)
            real = product[pl.ds(start, 8), own]
            imag = product[pl.ds(SUB + start, 8), own]
            if digit:
                cos = jnp.broadcast_to(twiddle[:, digit : digit + 1], (8, LANES))
                sin = jnp.broadcast_to(twiddle[:, RADIX + digit : RADIX + digit + 1], (8, LANES))
                real, imag = real * cos - imag * sin, real * sin + imag * cos
            turned.append((real, imag))
        even, odd = dft8(turned[0::2]), dft8(turned[1::2])
        first_row = row_ids + (step * 8).astype(jnp.float32)
        for high_digit in range(HALF_RADIX):
            angle = 2.0 * math.pi * high_digit / RADIX
            cos, sin = sign * math.cos(angle), sign * -math.sin(angle)
            e, o = even[high_digit], odd[high_digit]
            real = e[0] + (o[0] * cos - o[1] * sin)
            imag = e[1] + (o[0] * sin + o[1] * cos)
            along_x = first_row + float(high_digit * SUB)
            inverse = 1.0 / (along_x * along_x + cross)
            along = jnp.where(low, along_x, along_y)
            scaled = along * inverse
            dot_real, dot_imag = along * real, along * imag
            dot_real = dot_real + swap_halves(dot_real)
            dot_imag = dot_imag + swap_halves(dot_imag)
            result[high_digit, 0, pl.ds(start, 8), :] = real - scaled * dot_real
            result[high_digit, 1, pl.ds(start, 8), :] = imag - scaled * dot_imag
        return carry

    lax.fori_loop(0, SUB // 8, rows_body, 0)
    copies = []
    for step in range(side_size):
        owner = lax.bitwise_xor(own_place, step)
        copies.append(
            pltpu.make_async_copy(
                result.at[pl.ds(owner * per_owner, per_owner)], outs[step], sems.at[step]
            )
        )
    for copy in copies:
        copy.start()
    for copy in copies:
        copy.wait()


def transform(meta, waves, tables, lines, side_size):
    per_owner = HALF_RADIX // side_size
    vmem = pl.BlockSpec(memory_space=pltpu.VMEM)
    block = jax.ShapeDtypeStruct((per_owner, 2, SUB, LANES), jnp.float32)
    return pl.pallas_call(
        functools.partial(transform_kernel, side_size=side_size),
        in_specs=[pl.BlockSpec(memory_space=pltpu.SMEM)] + [vmem] * 5,
        out_specs=[pl.BlockSpec(memory_space=pl.ANY)] * side_size,
        out_shape=[block] * side_size,
        scratch_shapes=[
            pltpu.VMEM((SUB, RADIX * LANES), jnp.bfloat16),
            pltpu.VMEM((SUB, RADIX * LANES), jnp.bfloat16),
            pltpu.VMEM((2 * SUB, RADIX * LANES), jnp.float32),
            pltpu.VMEM((HALF_RADIX, 2, SUB, LANES), jnp.float32),
            pltpu.SemaphoreType.DMA((side_size,)),
        ],
        compiler_params=pltpu.CompilerParams(vmem_limit_bytes=32 * MIB),
        cost_estimate=pl.CostEstimate(
            flops=6 * 2 * SUB * SUB * RADIX * LANES, transcendentals=0, bytes_accessed=5 * MIB
        ),
        name="transform",
    )(meta, waves, *tables, lines)


def place_kernel(meta_ref, *refs, side_size):
    ins, out_ref = refs[:side_size], refs[-1]
    own_place = meta_ref[0]
    for part in range(2):
        held = [ref[0, part] for ref in ins]
        low = low_lanes(held[0].shape)
        blocks = []
        for source in range(side_size):
            step = lax.bitwise_xor(own_place, source)
            value = held[0]
            for other in range(1, side_size):
                value = jnp.where(step == other, held[other], value)
            blocks.append(value)
        for tile in range(side_size // 2):
            even, odd = blocks[2 * tile], blocks[2 * tile + 1]
            own = slice(tile * LANES, (tile + 1) * LANES)
            out_ref[0, part, :, own] = jnp.where(low, even, swap_halves(odd))
            out_ref[1, part, :, own] = jnp.where(low, swap_halves(even), odd)


def place(meta, blocks, before, chunk, pencils):
    side_size = len(blocks)
    per_owner = blocks[0].shape[0]
    rows = 64
    steps = SUB // rows
    width = side_size * HALF_LANES
    in_specs = [pl.BlockSpec(memory_space=pltpu.SMEM)]
    in_specs += [pl.BlockSpec((1, 2, rows, LANES), lambda q, r: (q, 0, r, 0))] * side_size
    operands = [meta, *blocks]
    aliases = {}
    if before is not None:
        in_specs.append(pl.BlockSpec(memory_space=pl.ANY))
        aliases = {len(operands): 0}
        operands.append(before)
    return pl.pallas_call(
        functools.partial(place_kernel, side_size=side_size),
        grid=(per_owner, steps),
        in_specs=in_specs,
        out_specs=pl.BlockSpec((2, 2, rows, width), lambda q, r: (0, 0, q * steps + r, chunk)),
        out_shape=jax.ShapeDtypeStruct((2, 2, per_owner * SUB, pencils), jnp.float32),
        input_output_aliases=aliases,
        cost_estimate=pl.CostEstimate(
            flops=0, transcendentals=0, bytes_accessed=8 * per_owner * 2 * SUB * LANES * side_size
        ),
        name="place",
    )(*operands)


def shards(packed, wave_y, wave_z):
    cycle_size = lax.axis_size("gx")
    side_size = cycle_size // 2
    pencils = packed.shape[2]
    chunks = pencils // (side_size * HALF_LANES)
    device_pos = lax.axis_index("gx")
    own_place = lax.rem(device_pos, side_size)
    side = device_pos // side_size
    meta = jnp.stack([own_place, side]).astype(jnp.int32)
    tables = [jnp.asarray(table) for table in dft_tables()]
    along_y = wave_y.astype(jnp.float32)
    along_z = wave_z.astype(jnp.float32)
    cross = along_y * along_y + along_z * along_z
    sends = [pack_lines(packed, chunk, side_size) for chunk in range(chunks)]
    lines = [
        lax.all_to_all(send, "gx", split_axis=0, concat_axis=0, tiled=True).reshape(NX, LANES)
        for send in sends
    ]
    result = None
    for chunk in range(chunks):
        start = (chunk * side_size + own_place) * HALF_LANES
        own_y = lax.dynamic_slice_in_dim(along_y, start, HALF_LANES)
        own_cross = lax.dynamic_slice_in_dim(cross, start, HALF_LANES)
        waves = jnp.stack([jnp.tile(own_y, 2), jnp.tile(own_cross, 2)])
        blocks = transform(meta, waves, tables, lines[chunk], side_size)
        blocks = [
            block
            if step == 0
            else lax.ppermute(block, "gx", [(i, i ^ step) for i in range(cycle_size)])
            for step, block in enumerate(blocks)
        ]
        result = place(meta, blocks, result, chunk, pencils)
    return result


def solution(mesh):
    return jax.shard_map(
        shards,
        mesh=mesh,
        in_specs=(P(None, "gx", "pa"), P("pa"), P("pa")),
        out_specs=P(None, None, "gx", "pa"),
        check_vma=False,
    )
```

```python
import functools
import math

import jax
import jax.numpy as jnp
import ml_dtypes
import numpy as np
from jax import lax
from jax.experimental import pallas as pl
from jax.experimental.pallas import tpu as pltpu
from jax.sharding import PartitionSpec as P

NX = 4096
RADIX = 16
SUB = NX // RADIX
HALF_RADIX = RADIX // 2
HALF_LANES = 64
LANES = 2 * HALF_LANES
MIB = 1 << 20


def dft_tables():
    rows = np.arange(SUB)
    angles = 2.0 * np.pi * (rows[:, None] * rows[None, :] % SUB) / SUB
    matrix = np.concatenate([np.cos(angles), -np.sin(angles)]) / math.sqrt(NX)
    high = matrix.astype(np.float32).astype(ml_dtypes.bfloat16)
    low = (matrix - high.astype(np.float64)).astype(np.float32).astype(ml_dtypes.bfloat16)
    turn = 2.0 * np.pi * rows[:, None] * np.arange(RADIX)[None, :] / NX
    twiddle = np.concatenate([np.cos(turn), -np.sin(turn)], axis=1).astype(np.float32)
    return high, low, twiddle


def low_lanes(shape):
    return lax.broadcasted_iota(jnp.int32, shape, len(shape) - 1) < HALF_LANES


def swap_halves(value):
    return pltpu.roll(value, HALF_LANES, value.ndim - 1)


def pack_kernel(meta_ref, in_hbm, *rest, side_size, plan):
    outs, (lines, mixed, sems) = rest[:-3], rest[-3:]
    tiles = side_size // 2
    chunks = sorted({chunk for targets in plan for _, chunk, _, _ in targets})
    loads = {}
    for chunk in chunks:
        for tile in range(tiles):
            columns = pl.ds((chunk * tiles + tile) * LANES, LANES)
            slot = len(loads)
            loads[chunk, tile] = pltpu.make_async_copy(
                in_hbm.at[:, :, columns], lines.at[slot], sems.at[slot]
            )
            loads[chunk, tile].start()
    stores = []
    for index, chunk in enumerate(chunks):
        for tile in range(tiles):
            loads[chunk, tile].wait()
            slot = index * tiles + tile
            first, second = lines[slot, 0], lines[slot, 1]
            low = low_lanes(first.shape)
            moved = swap_halves(jnp.where(low, second, first))
            mixed[index, 2 * tile] = jnp.where(low, first, moved)
            mixed[index, 2 * tile + 1] = jnp.where(low, moved, second)
        for out, targets in zip(outs, plan):
            for spot, own_chunk, owner, relative in targets:
                if own_chunk == chunk:
                    if relative:
                        owner = lax.bitwise_xor(meta_ref[0], owner)
                    stores.append(
                        pltpu.make_async_copy(
                            mixed.at[index, owner], out.at[spot], sems.at[len(loads) + len(stores)]
                        )
                    )
                    stores[-1].start()
    for store in stores:
        store.wait()


def pack_lines(meta, packed, side_size, plan, shapes):
    block_len = packed.shape[1]
    tiles = side_size // 2
    hbm = pl.BlockSpec(memory_space=pl.ANY)
    chunks = len({chunk for targets in plan for _, chunk, _, _ in targets})
    copies = sum(len(targets) for targets in plan)
    return pl.pallas_call(
        functools.partial(pack_kernel, side_size=side_size, plan=plan),
        in_specs=[pl.BlockSpec(memory_space=pltpu.SMEM), hbm],
        out_specs=[hbm] * len(plan),
        out_shape=[
            jax.ShapeDtypeStruct((*shape, block_len, LANES), jnp.float32) for shape in shapes
        ],
        scratch_shapes=[
            pltpu.VMEM((chunks * tiles, 2, block_len, LANES), jnp.float32),
            pltpu.VMEM((chunks, side_size, block_len, LANES), jnp.float32),
            pltpu.SemaphoreType.DMA((chunks * tiles + copies,)),
        ],
        cost_estimate=pl.CostEstimate(
            flops=0,
            transcendentals=0,
            bytes_accessed=4 * block_len * LANES * (chunks * side_size + copies),
        ),
        name="pack_lines",
    )(meta, packed)


def add(left, right):
    return left[0] + right[0], left[1] + right[1]


def sub(left, right):
    return left[0] - right[0], left[1] - right[1]


def turn_back(value):
    return value[1], -value[0]


def dft4(values):
    even_sum, even_dif = add(values[0], values[2]), sub(values[0], values[2])
    odd_sum, odd_dif = add(values[1], values[3]), turn_back(sub(values[1], values[3]))
    return [add(even_sum, odd_sum), add(even_dif, odd_dif), sub(even_sum, odd_sum), sub(even_dif, odd_dif)]


def dft8(values):
    root = math.sqrt(0.5)
    even, odd = dft4(values[0::2]), dft4(values[1::2])
    one = odd[1]
    three = odd[3]
    odd[1] = ((one[0] + one[1]) * root, (one[1] - one[0]) * root)
    odd[2] = turn_back(odd[2])
    odd[3] = ((three[1] - three[0]) * root, (three[0] + three[1]) * -root)
    return [add(e, o) for e, o in zip(even, odd)] + [sub(e, o) for e, o in zip(even, odd)]


def transform_kernel(
    meta_ref, wave_y_ref, wave_z_ref, high_ref, low_ref, twiddle_hbm, *rest, chunk, side_size, spots
):
    operands = 1 + max(operand for operand, _, _, _ in spots)
    inputs, rest = rest[:operands], rest[operands:]
    outs = rest[:side_size]
    split_high, split_low, product, result, twiddle, line, sems, line_sems = rest[side_size:]
    block_len = inputs[0].shape[-2]
    span = block_len // RADIX
    device_pos = meta_ref[1] * side_size + meta_ref[0]
    per_owner = HALF_RADIX // side_size
    load = pltpu.make_async_copy(twiddle_hbm, twiddle, sems.at[side_size])
    load.start()
    fetches, targets = [], []
    for step, (operand, spot, place, relative) in enumerate(spots):
        rows = pl.ds(place * span, span)
        if relative:
            source = lax.bitwise_xor(device_pos, place)
            fetches.append(
                pltpu.make_async_copy(
                    inputs[operand].at[spot], line.at[source], line_sems.at[step]
                )
            )
            fetches[-1].start()
            targets.append((line, place, rows))
        else:
            targets.append((inputs[operand], spot, rows))
    for fetch in fetches:
        fetch.wait()
    dot = functools.partial(jnp.dot, preferred_element_type=jnp.float32)
    for pair in range(RADIX // 2):
        columns = slice(2 * pair * LANES, 2 * (pair + 1) * LANES)
        for digit in (2 * pair, 2 * pair + 1):
            own = slice(digit * LANES, (digit + 1) * LANES)
            for ref, spot, rows in targets:
                value = ref[spot, pl.ds(digit, span, stride=RADIX), :]
                high = value.astype(jnp.bfloat16)
                split_high[rows, own] = high
                split_low[rows, own] = (value - high.astype(jnp.float32)).astype(jnp.bfloat16)
        product[:, columns] = (
            dot(high_ref[...], split_high[:, columns])
            + dot(high_ref[...], split_low[:, columns])
            + dot(low_ref[...], split_high[:, columns])
        )

    own_place = meta_ref[0]
    side_float = meta_ref[1].astype(jnp.float32)
    sign = 1.0 - 2.0 * side_float
    low = low_lanes((8, LANES))
    group = chunk * side_size + own_place
    keep = (lax.broadcasted_iota(jnp.int32, (1, LANES), 1) < HALF_LANES) == (group % 2 == 0)

    def own_lanes(ref):
        tile = ref[pl.ds(group // 2, 1), :].astype(jnp.float32)
        return jnp.where(keep, tile, swap_halves(tile))

    own_y, own_z = own_lanes(wave_y_ref), own_lanes(wave_z_ref)
    along_y = jnp.broadcast_to(own_y, (8, LANES))
    cross = jnp.broadcast_to(own_y * own_y + own_z * own_z, (8, LANES))
    row_ids = lax.broadcasted_iota(jnp.int32, (8, LANES), 0).astype(jnp.float32) - 2048.0 * side_float
    load.wait()

    def rows_body(step, carry):
        start = pl.multiple_of(step * 8, 8)
        turned = []
        for digit in range(RADIX):
            own = slice(digit * LANES, (digit + 1) * LANES)
            real = product[pl.ds(start, 8), own]
            imag = product[pl.ds(SUB + start, 8), own]
            if digit:
                cos = twiddle[digit, pl.ds(start, 8), :]
                sin = twiddle[RADIX + digit, pl.ds(start, 8), :]
                real, imag = real * cos - imag * sin, real * sin + imag * cos
            turned.append((real, imag))
        even, odd = dft8(turned[0::2]), dft8(turned[1::2])
        first_row = row_ids + (step * 8).astype(jnp.float32)
        for high_digit in range(HALF_RADIX):
            angle = 2.0 * math.pi * high_digit / RADIX
            cos, sin = sign * math.cos(angle), sign * -math.sin(angle)
            e, o = even[high_digit], odd[high_digit]
            real = e[0] + (o[0] * cos - o[1] * sin)
            imag = e[1] + (o[0] * sin + o[1] * cos)
            along_x = first_row + float(high_digit * SUB)
            inverse = 1.0 / (along_x * along_x + cross)
            along = jnp.where(low, along_x, along_y)
            scaled = along * inverse
            dot_real, dot_imag = along * real, along * imag
            dot_real = dot_real + swap_halves(dot_real)
            dot_imag = dot_imag + swap_halves(dot_imag)
            result[high_digit, 0, pl.ds(start, 8), :] = real - scaled * dot_real
            result[high_digit, 1, pl.ds(start, 8), :] = imag - scaled * dot_imag
        return carry

    copies = []
    parts = 2
    for part in range(parts):
        steps = SUB // 8 // parts
        lax.fori_loop(part * steps, (part + 1) * steps, rows_body, 0, unroll=UNROLL)
        rows = pl.ds(part * SUB // parts, SUB // parts)
        for step in range(side_size):
            owner = lax.bitwise_xor(own_place, step)
            copies.append(
                pltpu.make_async_copy(
                    result.at[pl.ds(owner * per_owner, per_owner), :, rows],
                    outs[step].at[:, :, rows],
                    sems.at[step + part * (side_size + 1)],
                )
            )
            copies[-1].start()
    for copy in copies:
        copy.wait()


UNROLL = 4


def transform(meta, wave_y, wave_z, tables, arrays, spots, chunk, side_size):
    per_owner = HALF_RADIX // side_size
    vmem = pl.BlockSpec(memory_space=pltpu.VMEM)
    hbm = pl.BlockSpec(memory_space=pl.ANY)
    block = jax.ShapeDtypeStruct((per_owner, 2, SUB, LANES), jnp.float32)
    return pl.pallas_call(
        functools.partial(transform_kernel, chunk=chunk, side_size=side_size, spots=spots),
        in_specs=[pl.BlockSpec(memory_space=pltpu.SMEM)] + [vmem] * 4 + [hbm] + [vmem] * len(arrays),
        out_specs=[hbm] * side_size,
        out_shape=[block] * side_size,
        scratch_shapes=[
            pltpu.VMEM((SUB, RADIX * LANES), jnp.bfloat16),
            pltpu.VMEM((SUB, RADIX * LANES), jnp.bfloat16),
            pltpu.VMEM((2 * SUB, RADIX * LANES), jnp.float32),
            pltpu.VMEM((HALF_RADIX, 2, SUB, LANES), jnp.float32),
            pltpu.VMEM((2 * RADIX, SUB, LANES), jnp.float32),
            pltpu.VMEM((2 * side_size, NX // (2 * side_size), LANES), jnp.float32),
            pltpu.SemaphoreType.DMA((2 * side_size + 1,)),
            pltpu.SemaphoreType.DMA((2 * side_size,)),
        ],
        compiler_params=pltpu.CompilerParams(vmem_limit_bytes=24 * MIB),
        cost_estimate=pl.CostEstimate(
            flops=6 * 2 * SUB * SUB * RADIX * LANES, transcendentals=0, bytes_accessed=5 * MIB
        ),
        name="transform",
    )(meta, wave_y, wave_z, *tables, *arrays)


def place_kernel(meta_ref, even_ref, odd_ref, *rest, chunk, step, side_size):
    out_hbm, mixed, sems = rest[-3:]
    own_place = meta_ref[0]
    tile = chunk * (side_size // 2) + lax.bitwise_xor(own_place // 2, step)
    ordered = own_place % 2 == 0
    columns = pl.ds(pl.multiple_of(tile * LANES, LANES), LANES)
    rows = SUB // PARTS
    stores = []
    for part in range(mixed.shape[0] * PARTS):
        index, own = part // PARTS, pl.ds(part % PARTS * rows, rows)
        first, second = even_ref[index, :, own], odd_ref[index, :, own]
        even = jnp.where(ordered, first, second)
        odd = jnp.where(ordered, second, first)
        low = low_lanes(even.shape)
        moved = swap_halves(jnp.where(low, odd, even))
        mixed[index, 0, :, own] = jnp.where(low, even, moved)
        mixed[index, 1, :, own] = jnp.where(low, moved, odd)
        stores.append(
            pltpu.make_async_copy(
                mixed.at[index, :, :, own],
                out_hbm.at[:, :, pl.ds(part * rows, rows), columns],
                sems.at[part],
            )
        )
        stores[-1].start()
    for store in stores:
        store.wait()


PARTS = 2


def place(meta, pair, before, chunk, step, side_size, pencils):
    per_owner = pair[0].shape[0]
    vmem = pl.BlockSpec(memory_space=pltpu.VMEM)
    hbm = pl.BlockSpec(memory_space=pl.ANY)
    operands = [meta, *pair]
    aliases = {}
    if before is not None:
        aliases = {len(operands): 0}
        operands.append(before)
    return pl.pallas_call(
        functools.partial(place_kernel, chunk=chunk, step=step, side_size=side_size),
        in_specs=[pl.BlockSpec(memory_space=pltpu.SMEM)] + [vmem] * 2 + [hbm] * (len(operands) - 3),
        out_specs=hbm,
        out_shape=jax.ShapeDtypeStruct((2, 2, per_owner * SUB, pencils), jnp.float32),
        scratch_shapes=[
            pltpu.VMEM((per_owner, 2, 2, SUB, LANES), jnp.float32),
            pltpu.SemaphoreType.DMA((PARTS * per_owner,)),
        ],
        input_output_aliases=aliases,
        compiler_params=pltpu.CompilerParams(vmem_limit_bytes=8 * MIB),
        cost_estimate=pl.CostEstimate(
            flops=0, transcendentals=0, bytes_accessed=16 * per_owner * 2 * SUB * LANES
        ),
        name="place",
    )(*operands)


def shards(packed, wave_y, wave_z):
    cycle_size = lax.axis_size("gx")
    side_size = cycle_size // 2
    block_len, pencils = packed.shape[1:]
    chunks = pencils // (side_size * HALF_LANES)
    device_pos = lax.axis_index("gx")
    own_place = lax.rem(device_pos, side_size)
    side = device_pos // side_size
    meta = jnp.stack([own_place, side]).astype(jnp.int32)
    high, low, twiddle = dft_tables()
    twiddle = jnp.broadcast_to(jnp.asarray(twiddle.T)[:, :, None], (2 * RADIX, SUB, LANES))
    tables = [jnp.asarray(high), jnp.asarray(low), twiddle]
    wave_y = wave_y.reshape(pencils // LANES, LANES)
    wave_z = wave_z.reshape(pencils // LANES, LANES)

    def swap(value, step):
        return lax.ppermute(value, "gx", [(i, i ^ step) for i in range(cycle_size)])

    places = list(range(side_size))
    first_plan = [[((side, place), 0, place, False) for side in range(2) for place in places]]
    (send,) = pack_lines(meta, packed, side_size, first_plan, [(2, side_size)])
    got = lax.all_to_all(
        send.reshape(cycle_size, block_len, LANES), "gx", split_axis=0, concat_axis=0, tiled=True
    )
    lines = [([got], [(0, place, place, False) for place in range(cycle_size)])]
    for chunk in range(1, chunks):
        (send,), packed = lax.optimization_barrier(((send,), packed))
        near_plan = [[(0, chunk, place, True)] for place in places]
        near = pack_lines(meta, packed, side_size, near_plan, [(1,)] * side_size)
        near = [near[0]] + [swap(near[place], place) for place in places[1:]]
        held = jnp.concatenate(near)
        got, held = lax.optimization_barrier((got, held))
        lines[0] = ([got], lines[0][1])
        far = swap(held, side_size)
        spots = [(0, place, place, True) for place in places]
        spots += [(1, place, side_size + place, True) for place in places]
        lines.append(([held, far], spots))
    result = None
    for chunk in range(chunks):
        blocks = transform(meta, wave_y, wave_z, tables, *lines[chunk], chunk, side_size)
        blocks = [
            block
            if step == 0
            else lax.ppermute(block, "gx", [(i, i ^ step) for i in range(cycle_size)])
            for step, block in enumerate(blocks)
        ]
        for step in range(side_size // 2):
            pair = blocks[2 * step : 2 * step + 2]
            result = place(meta, pair, result, chunk, step, side_size, pencils)
    return result


def solution(mesh):
    return jax.shard_map(
        shards,
        mesh=mesh,
        in_specs=(P(None, "gx", "pa"), P("pa"), P("pa")),
        out_specs=P(None, None, "gx", "pa"),
        check_vma=False,
    )
```

```python
import functools
import math

import jax
import jax.numpy as jnp
import ml_dtypes
import numpy as np
from jax import lax
from jax.experimental import pallas as pl
from jax.experimental.pallas import tpu as pltpu
from jax.sharding import PartitionSpec as P

NX = 4096
RADIX = 16
SUB = NX // RADIX
HALF_RADIX = RADIX // 2
HALF_LANES = 64
LANES = 2 * HALF_LANES
MIB = 1 << 20


def dft_tables():
    rows = np.arange(SUB)
    angles = 2.0 * np.pi * (rows[:, None] * rows[None, :] % SUB) / SUB
    matrix = np.concatenate([np.cos(angles), -np.sin(angles)]) / math.sqrt(NX)
    high = matrix.astype(np.float32).astype(ml_dtypes.bfloat16)
    low = (matrix - high.astype(np.float64)).astype(np.float32).astype(ml_dtypes.bfloat16)
    turn = 2.0 * np.pi * rows[:, None] * np.arange(RADIX)[None, :] / NX
    twiddle = np.concatenate([np.cos(turn), -np.sin(turn)], axis=1).astype(np.float32)
    return high, low, twiddle


def low_lanes(shape):
    return lax.broadcasted_iota(jnp.int32, shape, len(shape) - 1) < HALF_LANES


def swap_halves(value):
    return pltpu.roll(value, HALF_LANES, value.ndim - 1)


def pack_kernel(*refs, side_size, plan):
    meta_ref, in_hbm = refs[0], refs[-len(plan) - 4]
    outs, (lines, mixed, sems) = refs[-len(plan) - 3 : -3], refs[-3:]
    tiles = side_size // 2
    chunks = sorted({chunk for targets in plan for _, chunk, _, _ in targets})
    loads = {}
    for chunk in chunks:
        for tile in range(tiles):
            columns = pl.ds((chunk * tiles + tile) * LANES, LANES)
            slot = len(loads)
            loads[chunk, tile] = pltpu.make_async_copy(
                in_hbm.at[:, :, columns], lines.at[slot], sems.at[slot]
            )
            loads[chunk, tile].start()
    stores = []
    for index, chunk in enumerate(chunks):
        for tile in range(tiles):
            loads[chunk, tile].wait()
            slot = index * tiles + tile
            first, second = lines[slot, 0], lines[slot, 1]
            low = low_lanes(first.shape)
            moved = swap_halves(jnp.where(low, second, first))
            mixed[index, 2 * tile] = jnp.where(low, first, moved)
            mixed[index, 2 * tile + 1] = jnp.where(low, moved, second)
        for out, targets in zip(outs, plan):
            for spot, own_chunk, owner, relative in targets:
                if own_chunk == chunk:
                    if relative:
                        owner = lax.bitwise_xor(meta_ref[0], owner)
                    stores.append(
                        pltpu.make_async_copy(
                            mixed.at[index, owner], out.at[spot], sems.at[len(loads) + len(stores)]
                        )
                    )
                    stores[-1].start()
    for store in stores:
        store.wait()


def pack_lines(meta, packed, side_size, plan, shapes):
    block_len = packed.shape[1]
    tiles = side_size // 2
    hbm = pl.BlockSpec(memory_space=pl.ANY)
    chunks = len({chunk for targets in plan for _, chunk, _, _ in targets})
    copies = sum(len(targets) for targets in plan)
    relative = any(target[3] for targets in plan for target in targets)
    return pl.pallas_call(
        functools.partial(pack_kernel, side_size=side_size, plan=plan),
        in_specs=[pl.BlockSpec(memory_space=pltpu.SMEM)] * relative + [hbm],
        out_specs=[hbm] * len(plan),
        out_shape=[
            jax.ShapeDtypeStruct((*shape, block_len, LANES), jnp.float32) for shape in shapes
        ],
        scratch_shapes=[
            pltpu.VMEM((chunks * tiles, 2, block_len, LANES), jnp.float32),
            pltpu.VMEM((chunks, side_size, block_len, LANES), jnp.float32),
            pltpu.SemaphoreType.DMA((chunks * tiles + copies,)),
        ],
        cost_estimate=pl.CostEstimate(
            flops=0,
            transcendentals=0,
            bytes_accessed=4 * block_len * LANES * (chunks * side_size + copies),
        ),
        name="pack_lines",
    )(*[meta] * relative, packed)


def add(left, right):
    return left[0] + right[0], left[1] + right[1]


def sub(left, right):
    return left[0] - right[0], left[1] - right[1]


def turn_back(value):
    return value[1], -value[0]


def dft4(values):
    even_sum, even_dif = add(values[0], values[2]), sub(values[0], values[2])
    odd_sum, odd_dif = add(values[1], values[3]), turn_back(sub(values[1], values[3]))
    return [add(even_sum, odd_sum), add(even_dif, odd_dif), sub(even_sum, odd_sum), sub(even_dif, odd_dif)]


def dft8(values):
    root = math.sqrt(0.5)
    even, odd = dft4(values[0::2]), dft4(values[1::2])
    one = odd[1]
    three = odd[3]
    odd[1] = ((one[0] + one[1]) * root, (one[1] - one[0]) * root)
    odd[2] = turn_back(odd[2])
    odd[3] = ((three[1] - three[0]) * root, (three[0] + three[1]) * -root)
    return [add(e, o) for e, o in zip(even, odd)] + [sub(e, o) for e, o in zip(even, odd)]


def contract(matrices, start, depth, blocks, split_high, split_low, store):
    span = depth // len(blocks)
    high, low = (ref[:, pl.ds(start, depth)] for ref in matrices)
    dot = functools.partial(jnp.dot, preferred_element_type=jnp.float32)
    for pair in range(RADIX // 2):
        columns = slice(2 * pair * LANES, 2 * (pair + 1) * LANES)
        for digit in (2 * pair, 2 * pair + 1):
            own = slice(digit * LANES, (digit + 1) * LANES)
            for place, (ref, index) in enumerate(blocks):
                rows = slice(place * span, (place + 1) * span)
                value = ref[index, pl.ds(digit, span, stride=RADIX), :]
                top = value.astype(jnp.bfloat16)
                split_high[rows, own] = top
                split_low[rows, own] = (value - top.astype(jnp.float32)).astype(jnp.bfloat16)
        total = dot(high, split_high[:, columns]) + dot(high, split_low[:, columns])
        store(columns, total + dot(low, split_high[:, columns]))


def begin_kernel(meta_ref, high_ref, low_ref, near_ref, out_ref, split_high, split_low):
    side_size = near_ref.shape[0]
    depth = SUB // 2
    start = pl.multiple_of(meta_ref[1] * depth, depth)
    blocks = [(near_ref, lax.bitwise_xor(meta_ref[0], place)) for place in range(side_size)]

    def store(columns, value):
        out_ref[:, columns] = value

    contract((high_ref, low_ref), start, depth, blocks, split_high, split_low, store)


def begin(meta, tables, near):
    vmem = pl.BlockSpec(memory_space=pltpu.VMEM)
    return pl.pallas_call(
        begin_kernel,
        in_specs=[pl.BlockSpec(memory_space=pltpu.SMEM)] + [vmem] * 3,
        out_specs=vmem,
        out_shape=jax.ShapeDtypeStruct((2 * SUB, RADIX * LANES), jnp.float32),
        scratch_shapes=[pltpu.VMEM((SUB // 2, RADIX * LANES), jnp.bfloat16)] * 2,
        compiler_params=pltpu.CompilerParams(vmem_limit_bytes=16 * MIB),
        cost_estimate=pl.CostEstimate(
            flops=6 * SUB * SUB * RADIX * LANES, transcendentals=0, bytes_accessed=5 * MIB
        ),
        name="begin",
    )(meta, *tables[:2], near)


def transform_kernel(
    meta_ref, wave_y_ref, wave_z_ref, high_ref, low_ref, twiddle, *rest, chunk, side_size, begun
):
    count = 3 if begun else 1
    inputs, rest = rest[:count], rest[count:]
    outs = rest[:side_size]
    split_high, split_low, product, result, line, sems, line_sems = rest[side_size:]
    per_owner = HALF_RADIX // side_size
    if begun:
        depth = SUB // 2
        start = pl.multiple_of((1 - meta_ref[1]) * depth, depth)
        fetches = []
        for step in range(side_size):
            ref = inputs[2].at[step - 1] if step else inputs[1].at[0]
            spot = line.at[lax.bitwise_xor(meta_ref[0], step)]
            fetches.append(pltpu.make_async_copy(ref, spot, line_sems.at[step]))
            fetches[-1].start()
        for fetch in fetches:
            fetch.wait()
        blocks = [(line, place) for place in range(side_size)]
    else:
        depth, start = SUB, 0
        blocks = [(inputs[0], place) for place in range(2 * side_size)]

    def store(columns, value):
        product[:, columns] = inputs[0][:, columns] + value if begun else value

    contract((high_ref, low_ref), start, depth, blocks, split_high, split_low, store)

    own_place = meta_ref[0]
    side_float = meta_ref[1].astype(jnp.float32)
    sign = 1.0 - 2.0 * side_float
    low = low_lanes((8, LANES))
    group = chunk * side_size + own_place
    keep = (lax.broadcasted_iota(jnp.int32, (1, LANES), 1) < HALF_LANES) == (group % 2 == 0)

    def own_lanes(ref):
        tile = ref[pl.ds(group // 2, 1), :].astype(jnp.float32)
        return jnp.where(keep, tile, swap_halves(tile))

    own_y, own_z = own_lanes(wave_y_ref), own_lanes(wave_z_ref)
    along_y = jnp.broadcast_to(own_y, (8, LANES))
    cross = jnp.broadcast_to(own_y * own_y + own_z * own_z, (8, LANES))
    row_ids = lax.broadcasted_iota(jnp.int32, (8, LANES), 0).astype(jnp.float32) - 2048.0 * side_float

    def rows_body(step, carry):
        start = pl.multiple_of(step * 8, 8)
        turned = []
        for digit in range(RADIX):
            own = slice(digit * LANES, (digit + 1) * LANES)
            real = product[pl.ds(start, 8), own]
            imag = product[pl.ds(SUB + start, 8), own]
            if digit:
                cos = twiddle[digit, pl.ds(start, 8), :]
                sin = twiddle[RADIX + digit, pl.ds(start, 8), :]
                real, imag = real * cos - imag * sin, real * sin + imag * cos
            turned.append((real, imag))
        even, odd = dft8(turned[0::2]), dft8(turned[1::2])
        first_row = row_ids + (step * 8).astype(jnp.float32)
        for high_digit in range(HALF_RADIX):
            angle = 2.0 * math.pi * high_digit / RADIX
            cos, sin = sign * math.cos(angle), sign * -math.sin(angle)
            e, o = even[high_digit], odd[high_digit]
            real = e[0] + (o[0] * cos - o[1] * sin)
            imag = e[1] + (o[0] * sin + o[1] * cos)
            along_x = first_row + float(high_digit * SUB)
            inverse = 1.0 / (along_x * along_x + cross)
            along = jnp.where(low, along_x, along_y)
            scaled = along * inverse
            dot_real, dot_imag = along * real, along * imag
            dot_real = dot_real + swap_halves(dot_real)
            dot_imag = dot_imag + swap_halves(dot_imag)
            result[high_digit, 0, pl.ds(start, 8), :] = real - scaled * dot_real
            result[high_digit, 1, pl.ds(start, 8), :] = imag - scaled * dot_imag
        return carry

    copies = []
    parts = 2
    for part in range(parts):
        steps = SUB // 8 // parts
        lax.fori_loop(part * steps, (part + 1) * steps, rows_body, 0, unroll=4)
        rows = pl.ds(part * SUB // parts, SUB // parts)
        for step in range(side_size):
            owner = lax.bitwise_xor(own_place, step)
            copies.append(
                pltpu.make_async_copy(
                    result.at[pl.ds(owner * per_owner, per_owner), :, rows],
                    outs[step].at[:, :, rows],
                    sems.at[step + part * (side_size + 1)],
                )
            )
            copies[-1].start()
    for copy in copies:
        copy.wait()


def transform(meta, wave_y, wave_z, tables, arrays, chunk, side_size):
    per_owner = HALF_RADIX // side_size
    begun = len(arrays) == 3
    depth = SUB // 2 if begun else SUB
    vmem = pl.BlockSpec(memory_space=pltpu.VMEM)
    hbm = pl.BlockSpec(memory_space=pl.ANY)
    block = jax.ShapeDtypeStruct((per_owner, 2, SUB, LANES), jnp.float32)
    return pl.pallas_call(
        functools.partial(transform_kernel, chunk=chunk, side_size=side_size, begun=begun),
        in_specs=[pl.BlockSpec(memory_space=pltpu.SMEM)] + [vmem] * (5 + len(arrays)),
        out_specs=[hbm] * side_size,
        out_shape=[block] * side_size,
        scratch_shapes=[
            pltpu.VMEM((depth, RADIX * LANES), jnp.bfloat16),
            pltpu.VMEM((depth, RADIX * LANES), jnp.bfloat16),
            pltpu.VMEM((2 * SUB, RADIX * LANES), jnp.float32),
            pltpu.VMEM((HALF_RADIX, 2, SUB, LANES), jnp.float32),
            pltpu.VMEM((side_size, NX // (2 * side_size), LANES), jnp.float32),
            pltpu.SemaphoreType.DMA((2 * side_size + 1,)),
            pltpu.SemaphoreType.DMA((side_size,)),
        ],
        compiler_params=pltpu.CompilerParams(vmem_limit_bytes=24 * MIB),
        cost_estimate=pl.CostEstimate(
            flops=6 * 2 * SUB * SUB * RADIX * LANES, transcendentals=0, bytes_accessed=5 * MIB
        ),
        name="transform",
    )(meta, wave_y, wave_z, *tables, *arrays)


def place_kernel(meta_ref, even_ref, odd_ref, *rest, chunk, step, side_size):
    out_hbm, mixed, sems = rest[-3:]
    own_place = meta_ref[0]
    tile = chunk * (side_size // 2) + lax.bitwise_xor(own_place // 2, step)
    ordered = own_place % 2 == 0
    columns = pl.ds(pl.multiple_of(tile * LANES, LANES), LANES)
    rows = SUB // PARTS
    stores = []
    for part in range(mixed.shape[0] * PARTS):
        index, own = part // PARTS, pl.ds(part % PARTS * rows, rows)
        first, second = even_ref[index, :, own], odd_ref[index, :, own]
        even = jnp.where(ordered, first, second)
        odd = jnp.where(ordered, second, first)
        low = low_lanes(even.shape)
        moved = swap_halves(jnp.where(low, odd, even))
        mixed[index, 0, :, own] = jnp.where(low, even, moved)
        mixed[index, 1, :, own] = jnp.where(low, moved, odd)
        stores.append(
            pltpu.make_async_copy(
                mixed.at[index, :, :, own],
                out_hbm.at[:, :, pl.ds(part * rows, rows), columns],
                sems.at[part],
            )
        )
        stores[-1].start()
    for store in stores:
        store.wait()


PARTS = 2


def place(meta, pair, before, chunk, step, side_size, pencils):
    per_owner = pair[0].shape[0]
    vmem = pl.BlockSpec(memory_space=pltpu.VMEM)
    hbm = pl.BlockSpec(memory_space=pl.ANY)
    operands = [meta, *pair]
    aliases = {}
    if before is not None:
        aliases = {len(operands): 0}
        operands.append(before)
    return pl.pallas_call(
        functools.partial(place_kernel, chunk=chunk, step=step, side_size=side_size),
        in_specs=[pl.BlockSpec(memory_space=pltpu.SMEM)] + [vmem] * 2 + [hbm] * (len(operands) - 3),
        out_specs=hbm,
        out_shape=jax.ShapeDtypeStruct((2, 2, per_owner * SUB, pencils), jnp.float32),
        scratch_shapes=[
            pltpu.VMEM((per_owner, 2, 2, SUB, LANES), jnp.float32),
            pltpu.SemaphoreType.DMA((PARTS * per_owner,)),
        ],
        input_output_aliases=aliases,
        compiler_params=pltpu.CompilerParams(vmem_limit_bytes=8 * MIB),
        cost_estimate=pl.CostEstimate(
            flops=0, transcendentals=0, bytes_accessed=16 * per_owner * 2 * SUB * LANES
        ),
        name="place",
    )(*operands)


def shards(packed, wave_y, wave_z):
    cycle_size = lax.axis_size("gx")
    side_size = cycle_size // 2
    block_len, pencils = packed.shape[1:]
    chunks = pencils // (side_size * HALF_LANES)
    device_pos = lax.axis_index("gx")
    own_place = lax.rem(device_pos, side_size)
    side = device_pos // side_size
    meta = jnp.stack([own_place, side]).astype(jnp.int32)
    high, low, twiddle = dft_tables()
    twiddle = jnp.broadcast_to(jnp.asarray(twiddle.T)[:, :, None], (2 * RADIX, SUB, LANES))
    tables = [jnp.asarray(high), jnp.asarray(low), twiddle]
    wave_y = wave_y.reshape(pencils // LANES, LANES)
    wave_z = wave_z.reshape(pencils // LANES, LANES)

    def swap(value, step):
        return lax.ppermute(value, "gx", [(i, i ^ step) for i in range(cycle_size)])

    places = list(range(side_size))
    first_plan = [[((side, place), 0, place, False) for side in range(2) for place in places]]
    (send,) = pack_lines(meta, packed, side_size, first_plan, [(2, side_size)])
    got = lax.all_to_all(
        send.reshape(cycle_size, block_len, LANES), "gx", split_axis=0, concat_axis=0, tiled=True
    )
    lines = [[got]]
    for chunk in range(1, chunks):
        (send,), packed = lax.optimization_barrier(((send,), packed))
        near_plan = [[(0, chunk, place, True)] for place in places]
        sends = pack_lines(meta, packed, side_size, near_plan, [(1,)] * side_size)
        early = swap(sends[0], side_size)
        near = [swap(sends[place], place) for place in places[1:]]
        others = jnp.concatenate(near)
        got, others = lax.optimization_barrier((got, others))
        lines[0] = [got]
        held = jnp.concatenate([sends[0], others])
        lines.append([begin(meta, tables, held), early, swap(others, side_size)])
    result = None
    for chunk in range(chunks):
        blocks = transform(meta, wave_y, wave_z, tables, lines[chunk], chunk, side_size)
        blocks = [
            block
            if step == 0
            else lax.ppermute(block, "gx", [(i, i ^ step) for i in range(cycle_size)])
            for step, block in enumerate(blocks)
        ]
        for step in range(side_size // 2):
            pair = blocks[2 * step : 2 * step + 2]
            result = place(meta, pair, result, chunk, step, side_size, pencils)
    return result


def solution(mesh):
    return jax.shard_map(
        shards,
        mesh=mesh,
        in_specs=(P(None, "gx", "pa"), P("pa"), P("pa")),
        out_specs=P(None, None, "gx", "pa"),
        check_vma=False,
    )
```

```python
import functools
import math

import jax
import jax.numpy as jnp
import ml_dtypes
import numpy as np
from jax import lax
from jax.experimental import pallas as pl
from jax.experimental.pallas import tpu as pltpu
from jax.sharding import PartitionSpec as P

NX = 4096
RADIX = 16
SUB = NX // RADIX
HALF_RADIX = RADIX // 2
HALF_LANES = 64
LANES = 2 * HALF_LANES
MIB = 1 << 20


def dft_tables():
    rows = np.arange(SUB)
    angles = 2.0 * np.pi * (rows[:, None] * rows[None, :] % SUB) / SUB
    matrix = np.concatenate([np.cos(angles), -np.sin(angles)]) / math.sqrt(NX)
    high = matrix.astype(np.float32).astype(ml_dtypes.bfloat16)
    low = (matrix - high.astype(np.float64)).astype(np.float32).astype(ml_dtypes.bfloat16)
    turn = 2.0 * np.pi * rows[:, None] * np.arange(RADIX)[None, :] / NX
    twiddle = np.concatenate([np.cos(turn), -np.sin(turn)], axis=1).astype(np.float32)
    return high, low, twiddle


def low_lanes(shape):
    return lax.broadcasted_iota(jnp.int32, shape, len(shape) - 1) < HALF_LANES


def swap_halves(value):
    return pltpu.roll(value, HALF_LANES, value.ndim - 1)


def pack_kernel(*refs, side_size, plan):
    meta_ref, in_hbm = refs[0], refs[-len(plan) - 4]
    outs, (lines, mixed, sems) = refs[-len(plan) - 3 : -3], refs[-3:]
    tiles = side_size // 2
    chunks = sorted({chunk for targets in plan for _, chunk, _, _ in targets})
    part_len = lines.shape[2] // PACK_PARTS
    loads = {}
    for chunk in chunks:
        for tile in range(tiles):
            columns = pl.ds((chunk * tiles + tile) * LANES, LANES)
            for part in range(PACK_PARTS):
                rows = pl.ds(part * part_len, part_len)
                slot = len(loads)
                loads[chunk, tile, part] = pltpu.make_async_copy(
                    in_hbm.at[:, rows, columns],
                    lines.at[slot // PACK_PARTS, :, rows],
                    sems.at[slot],
                )
                loads[chunk, tile, part].start()
    stores = []

    def send(index, chunk, owners, rows):
        for out, targets in zip(outs, plan):
            for spot, own_chunk, owner, relative in targets:
                if own_chunk != chunk or relative != (owners is None):
                    continue
                if relative:
                    owner = lax.bitwise_xor(meta_ref[0], owner)
                elif owner not in owners:
                    continue
                source = mixed.at[index, owner, rows]
                sem = sems.at[len(loads) + len(stores)]
                stores.append(pltpu.make_async_copy(source, out.at[spot].at[rows], sem))
                stores[-1].start()

    for index, chunk in enumerate(chunks):
        for tile in range(tiles):
            for part in range(PACK_PARTS):
                rows = pl.ds(part * part_len, part_len)
                loads[chunk, tile, part].wait()
                slot = index * tiles + tile
                first, second = lines[slot, 0, rows], lines[slot, 1, rows]
                low = low_lanes(first.shape)
                moved = swap_halves(jnp.where(low, second, first))
                mixed[index, 2 * tile, rows] = jnp.where(low, first, moved)
                mixed[index, 2 * tile + 1, rows] = jnp.where(low, moved, second)
                send(index, chunk, (2 * tile, 2 * tile + 1), rows)
        send(index, chunk, None, pl.ds(0, lines.shape[2]))
    for store in stores:
        store.wait()


PACK_PARTS = 2


def pack_lines(meta, packed, side_size, plan, shapes):
    block_len = packed.shape[1]
    tiles = side_size // 2
    hbm = pl.BlockSpec(memory_space=pl.ANY)
    chunks = len({chunk for targets in plan for _, chunk, _, _ in targets})
    copies = sum(len(targets) for targets in plan)
    relative = any(target[3] for targets in plan for target in targets)
    return pl.pallas_call(
        functools.partial(pack_kernel, side_size=side_size, plan=plan),
        in_specs=[pl.BlockSpec(memory_space=pltpu.SMEM)] * relative + [hbm],
        out_specs=[hbm] * len(plan),
        out_shape=[
            jax.ShapeDtypeStruct((*shape, block_len, LANES), jnp.float32) for shape in shapes
        ],
        scratch_shapes=[
            pltpu.VMEM((chunks * tiles, 2, block_len, LANES), jnp.float32),
            pltpu.VMEM((chunks, side_size, block_len, LANES), jnp.float32),
            pltpu.SemaphoreType.DMA((PACK_PARTS * (chunks * tiles + copies),)),
        ],
        cost_estimate=pl.CostEstimate(
            flops=0,
            transcendentals=0,
            bytes_accessed=4 * block_len * LANES * (chunks * side_size + copies),
        ),
        name="pack_lines",
    )(*[meta] * relative, packed)


def add(left, right):
    return left[0] + right[0], left[1] + right[1]


def sub(left, right):
    return left[0] - right[0], left[1] - right[1]


def turn_back(value):
    return value[1], -value[0]


def dft4(values):
    even_sum, even_dif = add(values[0], values[2]), sub(values[0], values[2])
    odd_sum, odd_dif = add(values[1], values[3]), turn_back(sub(values[1], values[3]))
    return [add(even_sum, odd_sum), add(even_dif, odd_dif), sub(even_sum, odd_sum), sub(even_dif, odd_dif)]


def dft8(values):
    root = math.sqrt(0.5)
    even, odd = dft4(values[0::2]), dft4(values[1::2])
    one = odd[1]
    three = odd[3]
    odd[1] = ((one[0] + one[1]) * root, (one[1] - one[0]) * root)
    odd[2] = turn_back(odd[2])
    odd[3] = ((three[1] - three[0]) * root, (three[0] + three[1]) * -root)
    return [add(e, o) for e, o in zip(even, odd)] + [sub(e, o) for e, o in zip(even, odd)]


def contract(matrices, start, depth, blocks, split_high, split_low, store):
    span = depth // len(blocks)
    both = None
    if len(matrices) == 1:
        both = matrices[0][:, pl.ds(2 * start, 2 * depth)]
        high = matrices[0][:, pl.ds(2 * start, depth)]
    else:
        high, low = (ref[:, pl.ds(start, depth)] for ref in matrices)
    dot = functools.partial(jnp.dot, preferred_element_type=jnp.float32)
    for pair in range(RADIX // 2):
        columns = slice(2 * pair * LANES, 2 * (pair + 1) * LANES)
        for digit in (2 * pair, 2 * pair + 1):
            own = slice(digit * LANES, (digit + 1) * LANES)
            for place, (ref, index) in enumerate(blocks):
                rows = slice(place * span, (place + 1) * span)
                value = ref[index, pl.ds(digit, span, stride=RADIX), :]
                top = value.astype(jnp.bfloat16)
                split_high[rows, own] = top
                if both is not None:
                    split_high[pl.ds(depth + place * span, span), own] = top
                split_low[rows, own] = (value - top.astype(jnp.float32)).astype(jnp.bfloat16)
        if both is None:
            total = dot(high, split_high[:, columns]) + dot(high, split_low[:, columns])
            store(columns, total + dot(low, split_high[:, columns]))
        else:
            store(columns, dot(both, split_high[:, columns]) + dot(high, split_low[:, columns]))


def begin_kernel(meta_ref, both_ref, near_ref, out_ref, split_high, split_low):
    side_size = near_ref.shape[0]
    depth = SUB // 2
    start = pl.multiple_of(meta_ref[1] * depth, depth)
    blocks = [(near_ref, lax.bitwise_xor(meta_ref[0], place)) for place in range(side_size)]

    def store(columns, value):
        out_ref[:, columns] = value

    contract((both_ref,), start, depth, blocks, split_high, split_low, store)


def begin(meta, both, near):
    vmem = pl.BlockSpec(memory_space=pltpu.VMEM)
    return pl.pallas_call(
        begin_kernel,
        in_specs=[pl.BlockSpec(memory_space=pltpu.SMEM)] + [vmem] * 2,
        out_specs=vmem,
        out_shape=jax.ShapeDtypeStruct((2 * SUB, RADIX * LANES), jnp.float32),
        scratch_shapes=[
            pltpu.VMEM((SUB, RADIX * LANES), jnp.bfloat16),
            pltpu.VMEM((SUB // 2, RADIX * LANES), jnp.bfloat16),
        ],
        compiler_params=pltpu.CompilerParams(vmem_limit_bytes=16 * MIB),
        cost_estimate=pl.CostEstimate(
            flops=6 * SUB * SUB * RADIX * LANES, transcendentals=0, bytes_accessed=5 * MIB
        ),
        name="begin",
    )(meta, both, near)


def transform_kernel(
    meta_ref, wave_y_ref, wave_z_ref, high_ref, low_ref, twiddle, *rest, chunk, side_size, begun
):
    count = 3 if begun else 1
    inputs, rest = rest[:count], rest[count:]
    outs = rest[:side_size]
    split_high, split_low, product, result, line, sems, line_sems = rest[side_size:]
    per_owner = HALF_RADIX // side_size
    if begun:
        depth = SUB // 2
        start = pl.multiple_of((1 - meta_ref[1]) * depth, depth)
        fetches = []
        for step in range(side_size):
            ref = inputs[2].at[step - 1] if step else inputs[1].at[0]
            spot = line.at[lax.bitwise_xor(meta_ref[0], step)]
            fetches.append(pltpu.make_async_copy(ref, spot, line_sems.at[step]))
            fetches[-1].start()
        for fetch in fetches:
            fetch.wait()
        blocks = [(line, place) for place in range(side_size)]
    else:
        depth, start = SUB, 0
        blocks = [(inputs[0], place) for place in range(2 * side_size)]

    def store(columns, value):
        product[:, columns] = inputs[0][:, columns] + value if begun else value

    matrices = (high_ref,) if begun else (high_ref, low_ref)
    contract(matrices, start, depth, blocks, split_high, split_low, store)

    own_place = meta_ref[0]
    side_float = meta_ref[1].astype(jnp.float32)
    sign = 1.0 - 2.0 * side_float
    low = low_lanes((8, LANES))
    group = chunk * side_size + own_place
    keep = (lax.broadcasted_iota(jnp.int32, (1, LANES), 1) < HALF_LANES) == (group % 2 == 0)

    def own_lanes(ref):
        tile = ref[pl.ds(group // 2, 1), :].astype(jnp.float32)
        return jnp.where(keep, tile, swap_halves(tile))

    own_y, own_z = own_lanes(wave_y_ref), own_lanes(wave_z_ref)
    along_y = jnp.broadcast_to(own_y, (8, LANES))
    cross = jnp.broadcast_to(own_y * own_y + own_z * own_z, (8, LANES))
    row_ids = lax.broadcasted_iota(jnp.int32, (8, LANES), 0).astype(jnp.float32) - 2048.0 * side_float

    def rows_body(step, carry):
        start = pl.multiple_of(step * 8, 8)
        turned = []
        for digit in range(RADIX):
            own = slice(digit * LANES, (digit + 1) * LANES)
            real = product[pl.ds(start, 8), own]
            imag = product[pl.ds(SUB + start, 8), own]
            if digit:
                cos = twiddle[digit, pl.ds(start, 8), :]
                sin = twiddle[RADIX + digit, pl.ds(start, 8), :]
                real, imag = real * cos - imag * sin, real * sin + imag * cos
            turned.append((real, imag))
        even, odd = dft8(turned[0::2]), dft8(turned[1::2])
        first_row = row_ids + (step * 8).astype(jnp.float32)
        for high_digit in range(HALF_RADIX):
            angle = 2.0 * math.pi * high_digit / RADIX
            cos, sin = sign * math.cos(angle), sign * -math.sin(angle)
            e, o = even[high_digit], odd[high_digit]
            real = e[0] + (o[0] * cos - o[1] * sin)
            imag = e[1] + (o[0] * sin + o[1] * cos)
            along_x = first_row + float(high_digit * SUB)
            inverse = 1.0 / (along_x * along_x + cross)
            along = jnp.where(low, along_x, along_y)
            scaled = along * inverse
            dot_real, dot_imag = along * real, along * imag
            dot_real = dot_real + swap_halves(dot_real)
            dot_imag = dot_imag + swap_halves(dot_imag)
            result[high_digit, 0, pl.ds(start, 8), :] = real - scaled * dot_real
            result[high_digit, 1, pl.ds(start, 8), :] = imag - scaled * dot_imag
        return carry

    copies = []
    parts = 2
    for part in range(parts):
        steps = SUB // 8 // parts
        lax.fori_loop(part * steps, (part + 1) * steps, rows_body, 0, unroll=8)
        rows = pl.ds(part * SUB // parts, SUB // parts)
        for step in range(side_size):
            owner = lax.bitwise_xor(own_place, step)
            copies.append(
                pltpu.make_async_copy(
                    result.at[pl.ds(owner * per_owner, per_owner), :, rows],
                    outs[step].at[:, :, rows],
                    sems.at[step + part * (side_size + 1)],
                )
            )
            copies[-1].start()
    for copy in copies:
        copy.wait()


def transform(meta, wave_y, wave_z, tables, arrays, chunk, side_size):
    per_owner = HALF_RADIX // side_size
    begun = len(arrays) == 3
    depth = SUB // 2 if begun else SUB
    vmem = pl.BlockSpec(memory_space=pltpu.VMEM)
    hbm = pl.BlockSpec(memory_space=pl.ANY)
    block = jax.ShapeDtypeStruct((per_owner, 2, SUB, LANES), jnp.float32)
    return pl.pallas_call(
        functools.partial(transform_kernel, chunk=chunk, side_size=side_size, begun=begun),
        in_specs=[pl.BlockSpec(memory_space=pltpu.SMEM)] + [vmem] * (5 + len(arrays)),
        out_specs=[hbm] * side_size,
        out_shape=[block] * side_size,
        scratch_shapes=[
            pltpu.VMEM((SUB, RADIX * LANES), jnp.bfloat16),
            pltpu.VMEM((depth, RADIX * LANES), jnp.bfloat16),
            pltpu.VMEM((2 * SUB, RADIX * LANES), jnp.float32),
            pltpu.VMEM((HALF_RADIX, 2, SUB, LANES), jnp.float32),
            pltpu.VMEM((side_size, NX // (2 * side_size), LANES), jnp.float32),
            pltpu.SemaphoreType.DMA((2 * side_size + 1,)),
            pltpu.SemaphoreType.DMA((side_size,)),
        ],
        compiler_params=pltpu.CompilerParams(vmem_limit_bytes=24 * MIB),
        cost_estimate=pl.CostEstimate(
            flops=6 * 2 * SUB * SUB * RADIX * LANES, transcendentals=0, bytes_accessed=5 * MIB
        ),
        name="transform",
    )(meta, wave_y, wave_z, *tables, *arrays)


def place_kernel(meta_ref, even_ref, odd_ref, *rest, chunk, step, side_size):
    out_hbm, mixed, sems = rest[-3:]
    own_place = meta_ref[0]
    tile = chunk * (side_size // 2) + lax.bitwise_xor(own_place // 2, step)
    ordered = own_place % 2 == 0
    columns = pl.ds(pl.multiple_of(tile * LANES, LANES), LANES)
    rows = SUB // PARTS
    stores = []
    for part in range(mixed.shape[0] * PARTS):
        index, own = part // PARTS, pl.ds(part % PARTS * rows, rows)
        first, second = even_ref[index, :, own], odd_ref[index, :, own]
        even = jnp.where(ordered, first, second)
        odd = jnp.where(ordered, second, first)
        low = low_lanes(even.shape)
        moved = swap_halves(jnp.where(low, odd, even))
        mixed[index, 0, :, own] = jnp.where(low, even, moved)
        mixed[index, 1, :, own] = jnp.where(low, moved, odd)
        stores.append(
            pltpu.make_async_copy(
                mixed.at[index, :, :, own],
                out_hbm.at[:, :, pl.ds(part * rows, rows), columns],
                sems.at[part],
            )
        )
        stores[-1].start()
    for store in stores:
        store.wait()


PARTS = 2


def place(meta, pair, before, chunk, step, side_size, pencils):
    per_owner = pair[0].shape[0]
    vmem = pl.BlockSpec(memory_space=pltpu.VMEM)
    hbm = pl.BlockSpec(memory_space=pl.ANY)
    operands = [meta, *pair]
    aliases = {}
    if before is not None:
        aliases = {len(operands): 0}
        operands.append(before)
    return pl.pallas_call(
        functools.partial(place_kernel, chunk=chunk, step=step, side_size=side_size),
        in_specs=[pl.BlockSpec(memory_space=pltpu.SMEM)] + [vmem] * 2 + [hbm] * (len(operands) - 3),
        out_specs=hbm,
        out_shape=jax.ShapeDtypeStruct((2, 2, per_owner * SUB, pencils), jnp.float32),
        scratch_shapes=[
            pltpu.VMEM((per_owner, 2, 2, SUB, LANES), jnp.float32),
            pltpu.SemaphoreType.DMA((PARTS * per_owner,)),
        ],
        input_output_aliases=aliases,
        compiler_params=pltpu.CompilerParams(vmem_limit_bytes=8 * MIB),
        cost_estimate=pl.CostEstimate(
            flops=0, transcendentals=0, bytes_accessed=16 * per_owner * 2 * SUB * LANES
        ),
        name="place",
    )(*operands)


def shards(packed, wave_y, wave_z):
    cycle_size = lax.axis_size("gx")
    side_size = cycle_size // 2
    block_len, pencils = packed.shape[1:]
    chunks = pencils // (side_size * HALF_LANES)
    device_pos = lax.axis_index("gx")
    own_place = lax.rem(device_pos, side_size)
    side = device_pos // side_size
    meta = jnp.stack([own_place, side]).astype(jnp.int32)
    high, low, twiddle = dft_tables()
    twiddle = jnp.broadcast_to(jnp.asarray(twiddle.T)[:, :, None], (2 * RADIX, SUB, LANES))
    tables = [jnp.asarray(high), jnp.asarray(low), twiddle]
    halves = [
        table[:, part : part + SUB // 2] for part in (0, SUB // 2) for table in (high, low)
    ]
    both = jnp.asarray(np.concatenate(halves, axis=1))
    wave_y = wave_y.reshape(pencils // LANES, LANES)
    wave_z = wave_z.reshape(pencils // LANES, LANES)

    def swap(value, step):
        return lax.ppermute(value, "gx", [(i, i ^ step) for i in range(cycle_size)])

    places = list(range(side_size))
    first_plan = [[((side, place), 0, place, False) for side in range(2) for place in places]]
    (send,) = pack_lines(meta, packed, side_size, first_plan, [(2, side_size)])
    got = lax.all_to_all(
        send.reshape(cycle_size, block_len, LANES), "gx", split_axis=0, concat_axis=0, tiled=True
    )
    lines = [[got]]
    for chunk in range(1, chunks):
        (send,), packed = lax.optimization_barrier(((send,), packed))
        near_plan = [[(0, chunk, place, True)] for place in places]
        sends = pack_lines(meta, packed, side_size, near_plan, [(1,)] * side_size)
        early = swap(sends[0], side_size)
        near = [swap(sends[place], place) for place in places[1:]]
        others = jnp.concatenate(near)
        got, others = lax.optimization_barrier((got, others))
        lines[0] = [got]
        held = jnp.concatenate([sends[0], others])
        lines.append([begin(meta, both, held), early, swap(others, side_size)])
    result = None
    for chunk in range(chunks):
        own_tables = tables if chunk == 0 else [both, *tables[1:]]
        blocks = transform(meta, wave_y, wave_z, own_tables, lines[chunk], chunk, side_size)
        blocks = [
            block
            if step == 0
            else lax.ppermute(block, "gx", [(i, i ^ step) for i in range(cycle_size)])
            for step, block in enumerate(blocks)
        ]
        for step in range(side_size // 2):
            pair = blocks[2 * step : 2 * step + 2]
            result = place(meta, pair, result, chunk, step, side_size, pencils)
    return result


def solution(mesh):
    return jax.shard_map(
        shards,
        mesh=mesh,
        in_specs=(P(None, "gx", "pa"), P("pa"), P("pa")),
        out_specs=P(None, None, "gx", "pa"),
        check_vma=False,
    )
```
